32 devices in a mesh: layer: 8 (over z, x), front: 4 (over y, core).
Axes of the slice: x: 2, y: 2, z: 4, core: 2. Of those that a mesh axis runs over, the one named last changes fastest.
Arguments:
- u_factor: bfloat16 [8, 2, 1024, 2560], P('layer', None, None, 'front'), may hold values from -0.1875 to 0.1875
- vt_factor: bfloat16 [8, 2, 1024, 2560], P('layer', None, None, 'front'), may hold values from -0.1875 to 0.1875
- diagonal: float32 [8, 2, 1024], P('layer', None, 'front'), may hold values from 1.5 to 3
- transmit: float32 [8, 1024], P('layer', 'front'), may hold values from 0.3 to 0.97
- sources: float32 [8, 2, 8, 1024], P('layer', None, None, 'front'), may hold values from -6 to 6
Outputs:
- field: float32 [8, 2, 8, 1024], P('layer', None, None, 'front')
The draws below stay inside these ranges and needn't reach their ends.
All inputs are finite; a program needn't handle non-finite values.
Results may differ from the reference program's by a relative error of at most 0.0003.
Values may be sent and summed in bfloat16 or wider, within the bound.
No kernel may reach another device: no remote copies, remote signals or barrier semaphores. Data moves between devices by JAX's collectives and lax.ppermute only.
A program may use at most 64 MiB of HBM per device.

```python
import math
import jax
import jax.numpy as jnp
from jax import lax

QDEV = 256
INT_DEV = 640
RHS = 8
JACOBI = 3
LAYERS = 8
PLANE = 1024
INTER = 2560
N_FRONT = 4


def steps_of(stream_key, shape, cuts, low, largest):
    loudness, own = 1.0, jax.random.fold_in(stream_key, 6)
    for dim, blocks in cuts:
        steps = jnp.exp(jax.random.uniform(jax.random.fold_in(own, dim), (blocks,), jnp.float32, low / len(cuts), largest / len(cuts)))
        loudness = loudness * jnp.repeat(steps, shape[dim] // blocks).reshape([-1 if axis == dim else 1 for axis in range(len(shape))])
    return loudness


def noise(own_key, extent, width, most, shards=(), dtype=jnp.bfloat16):
    values = jax.random.normal(own_key, extent, jnp.float32) * width
    if len(shards) > 0:
        values = steps_of(own_key, extent, shards, -0.22, 0.18) * values
    return jnp.clip(values, min=-most, max=most).astype(dtype)


def setup_inputs(seed: int = 0) -> dict:
    keys = jax.random.split(jax.random.key(seed), 6)
    return {
        "u_factor": noise(keys[0], (LAYERS, 2, PLANE, INTER), (2 * QDEV + INT_DEV * N_FRONT // 4) ** -0.5, 0.1875, ((0, 8), (3, 4))),
        "vt_factor": noise(keys[1], (LAYERS, 2, PLANE, INTER), (2 * QDEV + INT_DEV * N_FRONT // 4) ** -0.5, 0.1875, ((0, 8), (3, 4))),
        "diagonal": jnp.clip(1.5 + 1.5 * jax.random.uniform(keys[2], (LAYERS, 2, PLANE), jnp.float32) ** steps_of(keys[2], (LAYERS, 2, PLANE), ((0, 8), (2, 4)), -0.2, 0.2), 1.5, 3.0),
        "transmit": jnp.clip(jnp.exp(math.log(0.97) - 1.17351359 * jax.random.uniform(keys[3], (LAYERS, PLANE), jnp.float32) ** steps_of(keys[3], (LAYERS, PLANE), ((0, 8), (1, 4)), -0.2, 0.2)), 0.3, 0.97),
        "sources": noise(keys[4], (LAYERS, 2, RHS, PLANE), 1.0, 6.0, ((0, 8), (3, 4)), jnp.float32),
    }


def complex_block_product(left, right):
    def contract(first, second):
        return jnp.einsum("nik,njk->nij", first, second, precision=lax.Precision.HIGHEST)
    real_part = contract(left[0], right[0]) - contract(left[1], right[1])
    imag_part = contract(left[0], right[1]) + contract(left[1], right[0])
    return jnp.stack([real_part, imag_part], axis=1)


def complex_divide(real_num, imag_num, diag_real, diag_imag):
    denominator = diag_real * diag_real + diag_imag * diag_imag
    return (real_num * diag_real + imag_num * diag_imag) / denominator, (imag_num * diag_real - real_num * diag_imag) / denominator


def apply_blocks(blocks, part_real, part_imag):
    rhs_count = part_real.shape[0]
    shaped_real = part_real.reshape(rhs_count, N_FRONT, QDEV)
    shaped_imag = part_imag.reshape(rhs_count, N_FRONT, QDEV)

    def contract(matrix, vector):
        return jnp.einsum("fij,rfj->rfi", matrix, vector, precision=lax.Precision.HIGHEST)
    out_real = contract(blocks[:, 0], shaped_real) - contract(blocks[:, 1], shaped_imag)
    out_imag = contract(blocks[:, 0], shaped_imag) + contract(blocks[:, 1], shaped_real)
    return out_real.reshape(rhs_count, PLANE), out_imag.reshape(rhs_count, PLANE)


def sweep_layer(blocks, diag_layer, trans_layer, source_layer, incoming):
    diag_real = diag_layer[0][None, :]
    diag_imag = diag_layer[1][None, :]
    gain = trans_layer[None, :]
    drive_real = source_layer[0] + gain * (diag_real * incoming[0] - diag_imag * incoming[1])
    drive_imag = source_layer[1] + gain * (diag_real * incoming[1] + diag_imag * incoming[0])
    state_real, state_imag = complex_divide(drive_real, drive_imag, diag_real, diag_imag)
    for sweep_count in range(JACOBI):
        mixed_real, mixed_imag = apply_blocks(blocks, state_real, state_imag)
        state_real, state_imag = complex_divide(drive_real + mixed_real, drive_imag + mixed_imag, diag_real, diag_imag)
    return jnp.stack([state_real, state_imag], axis=0)


def reference(u_factor, vt_factor, diagonal, transmit, sources):
    def layer_step(incoming, layer_data):
        u_layer, vt_layer, diag_layer, trans_layer, source_layer = layer_data
        left = u_layer.astype(jnp.float32).reshape(2, N_FRONT, QDEV, INTER)
        right = vt_layer.astype(jnp.float32).reshape(2, N_FRONT, QDEV, INTER)
        blocks = complex_block_product(left, right)
        solved = sweep_layer(blocks, diag_layer, trans_layer, source_layer, incoming)
        return solved, solved

    start_state = jnp.zeros((2, RHS, PLANE), jnp.float32)
    final_state, field = lax.scan(layer_step, start_state, (u_factor, vt_factor, diagonal, transmit, sources))
    return field
```

```python
import functools

import jax
import jax.numpy as jnp
from jax import lax
from jax.experimental import pallas as pl
from jax.experimental.pallas import tpu as pltpu
from jax.sharding import PartitionSpec as P

JACOBI = 3
LINK = jnp.float16
VMEM = pl.BlockSpec(memory_space=pltpu.VMEM)


def swapped(value, axis, mask):
    route = [(i, i ^ mask) for i in range(lax.axis_size(axis))]
    return lax.ppermute(value, axis, route)


def products_kernel(masks, u_hbm, vt_hbm, out_ref, u_buf, vt_buf, sems):
    me = lax.axis_index("front")
    cells = u_buf.shape[2]
    copies = []
    for place, mask in enumerate(masks):
        group = jnp.bitwise_xor(me, mask)
        rows = pl.ds(pl.multiple_of(group * cells, cells), cells)
        pair = (
            pltpu.make_async_copy(u_hbm.at[0, :, rows, :], u_buf.at[place], sems.at[0, place]),
            pltpu.make_async_copy(vt_hbm.at[0, :, rows, :], vt_buf.at[place], sems.at[1, place]),
        )
        for copy in pair:
            copy.start()
        copies.append(pair)

    def contract(first, second):
        return lax.dot_general(
            first, second, (((1,), (1,)), ((), ())), preferred_element_type=jnp.float32
        )

    for place, pair in enumerate(copies):
        for copy in pair:
            copy.wait()
        u_real, u_imag = u_buf[place, 0], u_buf[place, 1]
        v_real, v_imag = vt_buf[place, 0], vt_buf[place, 1]
        out_ref[place, 0] = contract(v_real, u_real) - contract(v_imag, u_imag)
        out_ref[place, 1] = contract(v_real, u_imag) + contract(v_imag, u_real)


def products(u_factor, vt_factor, masks, cells):
    inner = u_factor.shape[3]
    count = len(masks)
    return pl.pallas_call(
        functools.partial(products_kernel, masks),
        out_shape=jax.ShapeDtypeStruct((count, 2, cells, cells), jnp.float32),
        in_specs=[pl.BlockSpec(memory_space=pltpu.HBM)] * 2,
        out_specs=VMEM,
        scratch_shapes=[
            pltpu.VMEM((count, 2, cells, inner), u_factor.dtype),
            pltpu.VMEM((count, 2, cells, inner), vt_factor.dtype),
            pltpu.SemaphoreType.DMA((2, count)),
        ],
        compiler_params=pltpu.CompilerParams(vmem_limit_bytes=24 << 20),
        cost_estimate=pl.CostEstimate(
            flops=8 * count * cells * cells * inner,
            bytes_accessed=count * cells * (8 * inner + 8 * cells),
            transcendentals=0,
        ),
        name="products",
    )(u_factor, vt_factor)


def apply_block(high_ref, low_ref, real, imag):
    count, cells = real.shape
    state = jnp.concatenate([real, imag], axis=0)
    top = state.astype(jnp.bfloat16)
    rest = (state - top.astype(jnp.float32)).astype(jnp.bfloat16)
    both = jnp.concatenate([top, rest], axis=0)
    by_high = jnp.dot(both, high_ref[...], preferred_element_type=jnp.float32)
    by_low = jnp.dot(top, low_ref[...], preferred_element_type=jnp.float32)
    total = by_high[: 2 * count] + by_high[2 * count :] + by_low
    return (
        total[:count, :cells] - total[count:, cells:],
        total[:count, cells:] + total[count:, :cells],
    )


def solve(high_ref, low_ref, small, incoming):
    rhs = (small.shape[0] - 8) // 2
    diag_real = small[2 * rhs : 2 * rhs + 1]
    diag_imag = small[2 * rhs + 1 : 2 * rhs + 2]
    gain = small[2 * rhs + 2 : 2 * rhs + 3]
    scale = 1.0 / (diag_real * diag_real + diag_imag * diag_imag)
    inv_real, inv_imag = diag_real * scale, -diag_imag * scale
    h_real, h_imag = small[:rhs], small[rhs : 2 * rhs]
    if incoming is not None:
        in_real, in_imag = incoming
        h_real = h_real + gain * (diag_real * in_real - diag_imag * in_imag)
        h_imag = h_imag + gain * (diag_real * in_imag + diag_imag * in_real)

    def divided(real, imag):
        return real * inv_real - imag * inv_imag, real * inv_imag + imag * inv_real

    x_real, x_imag = divided(h_real, h_imag)
    for _ in range(JACOBI):
        mixed_real, mixed_imag = apply_block(high_ref, low_ref, x_real, x_imag)
        x_real, x_imag = divided(h_real + mixed_real, h_imag + mixed_imag)
    return x_real, x_imag


def both_layers(blocks_ref, small_ref, incoming, out_ref):
    first = solve(blocks_ref.at[0], blocks_ref.at[1], small_ref[0], incoming)
    second = solve(blocks_ref.at[2], blocks_ref.at[3], small_ref[1], first)
    out_ref[0, 0], out_ref[0, 1] = first
    out_ref[1, 0], out_ref[1, 1] = second


def start_kernel(own_ref, other_ref, small_own, small_partner, blocks_ref, small_ref, out_ref):
    odd = lax.rem(lax.axis_index("layer"), 2) == 1
    cells = own_ref.shape[1]
    for part in range(2):
        own, other = own_ref[part], other_ref[part]
        columns = slice(part * cells, (part + 1) * cells)
        for place, block in enumerate((jnp.where(odd, other, own), jnp.where(odd, own, other))):
            high = block.astype(jnp.bfloat16)
            blocks_ref[2 * place, :, columns] = high
            blocks_ref[2 * place + 1, :, columns] = (block - high.astype(jnp.float32)).astype(
                jnp.bfloat16
            )
    small_ref[0] = jnp.where(odd, small_partner[...], small_own[...])
    small_ref[1] = jnp.where(odd, small_own[...], small_partner[...])
    both_layers(blocks_ref, small_ref, None, out_ref)


def hop_kernel(hop, blocks_ref, small_ref, came, current, out_ref):
    pair = lax.axis_index("layer") // 2

    @pl.when(pair == hop)
    def _():
        both_layers(blocks_ref, small_ref, (came[0], came[1]), out_ref)

    @pl.when(pair != hop)
    def _():
        out_ref[...] = current[...]


def shards(u_factor, vt_factor, diagonal, transmit, sources):
    cells = diagonal.shape[2]
    rhs = sources.shape[2]
    fronts = lax.axis_size("front")
    layers = lax.axis_size("layer")
    limit = pltpu.CompilerParams(vmem_limit_bytes=16 << 20)

    small_own = jnp.concatenate(
        [
            sources[0].reshape(2 * rhs, cells),
            diagonal[0],
            transmit,
            jnp.zeros((5, cells), jnp.float32),
        ],
        axis=0,
    )
    small_partner = swapped(small_own, "layer", 1)

    half = fronts // 2
    masks = list(range(half, fronts)), list(range(half))
    far = products(u_factor, vt_factor, masks[0], cells)
    near = products(u_factor, vt_factor, masks[1], cells)
    terms = {m: far[i] for i, m in enumerate(masks[0])}
    terms.update({m: near[i] for i, m in enumerate(masks[1])})
    for m in range(fronts - 1, -1, -1):
        if m & 1:
            terms[m ^ 1] = terms[m ^ 1] + swapped(terms[m], "front", 1)
    bit = half
    arrived = None
    while bit > 1:
        for m in range(0, bit, 2):
            arrived = swapped(terms[m + bit].astype(LINK), "front", bit)
            if bit > 2 or m:
                terms[m] = terms[m] + arrived.astype(jnp.float32)
        bit //= 2
    own = terms[0] + arrived.astype(jnp.float32)
    other = swapped(own.astype(LINK), "layer", 1).astype(jnp.float32)

    blocks, small, fields = pl.pallas_call(
        start_kernel,
        out_shape=(
            jax.ShapeDtypeStruct((4, cells, 2 * cells), jnp.bfloat16),
            jax.ShapeDtypeStruct((2,) + small_own.shape, jnp.float32),
            jax.ShapeDtypeStruct((2, 2, rhs, cells), jnp.float32),
        ),
        in_specs=[VMEM] * 4,
        out_specs=(VMEM,) * 3,
        compiler_params=limit,
        name="start",
    )(own, other, small_own, small_partner)

    for hop in range(1, layers // 2):
        route = [(2 * hop - 2 + x, 2 * hop + x) for x in range(2)]
        came = lax.ppermute(fields[1], "layer", route)
        fields = pl.pallas_call(
            functools.partial(hop_kernel, hop),
            out_shape=jax.ShapeDtypeStruct((2, 2, rhs, cells), jnp.float32),
            in_specs=[VMEM] * 4,
            out_specs=VMEM,
            compiler_params=limit,
            name=f"hop{hop}",
        )(blocks, small, came, fields)
    odd = lax.rem(lax.axis_index("layer"), 2) == 1
    return jnp.where(odd, fields[1], fields[0])[None]


def solution(mesh):
    placed = (
        P("layer", None, None, "front"),
        P("layer", None, None, "front"),
        P("layer", None, "front"),
        P("layer", "front"),
        P("layer", None, None, "front"),
    )
    return jax.shard_map(
        shards,
        mesh=mesh,
        in_specs=placed,
        out_specs=P("layer", None, None, "front"),
        check_vma=False,
    )
```
